768 devices in a mesh: ctx: 24 (over x_lo, z), tp: 32 (over y, x_hi, core).
Axes of the slice: x: 4 (x_hi: 2, x_lo: 2; x = x_hi * 2 + x_lo), y: 8, z: 12, core: 2. Of those that a mesh axis runs over, the one named last changes fastest.
Arguments:
- query_stream: bfloat16 [6144, 8192], P('ctx', 'tp'), may hold values from -6 to 6
- key_stream: bfloat16 [6144, 8192], P('ctx', 'tp'), may hold values from -6 to 6
- value_stream: bfloat16 [6144, 8192], P('ctx', 'tp'), may hold values from -6 to 6
- short_filter: float32 [3, 7, 8192], P(None, None, 'tp'), may hold values from -2 to 2
- long_filter: bfloat16 [512, 128], P('tp'), may hold values from -0.5 to 0.5
- doc_start: int32 [6144], P('ctx'), may hold values from 0 to 6143, as said below
- out_weight: bfloat16 [8192, 8192], P('tp'), may hold values from -0.0625 to 0.0625
- out_cotangent: bfloat16 [6144, 8192], P(('ctx', 'tp')), may hold values from -6 to 6
Outputs:
- projected: bfloat16 [6144, 8192], P(('ctx', 'tp'))
- stream_grads: bfloat16 [3, 6144, 8192], P(None, 'ctx', 'tp')
The draws below stay inside these ranges and needn't reach their ends.
Inputs may be any that keep to these rules, and one draw needn't show every extreme that they name: doc_start[t] is the first position of the document that holds position t: doc_start[0] = 0, doc_start[t] <= t, and doc_start[t] is either t or doc_start[t - 1]; the last position begins a document of its own.
All inputs are finite; a program needn't handle non-finite values.
Results may differ from the reference program's by a relative error of at most 0.015.
Values may be sent and summed in bfloat16 or wider, within the bound.
No kernel may reach another device: no remote copies, remote signals or barrier semaphores. Data moves between devices by JAX's collectives and lax.ppermute only.
A program may use at most 32 MiB of HBM per device.

```python
import jax
import jax.numpy as jnp
from jax import lax

D = 8192
GRP = 16
LONG = 128
SHORT = 7
TOK_DEV = 256
SEQ = 6144
GROUPS = 512
N_TP = 32


def draw_doc_start(key, part):
    positions = jnp.arange(SEQ, dtype=jnp.int32)
    boundary = jax.random.randint(jax.random.fold_in(key, 17), (SEQ,), 0, 2 * TOK_DEV) == 0
    boundary = jnp.logical_or(boundary, positions == 0)
    boundary = jnp.logical_or(boundary, positions == SEQ - 1)
    return lax.cummax(jnp.where(boundary, positions, 0), axis=0).astype(jnp.int32)


def levels(stream_key, dims, cuts, smallest, top_value):
    loudness, own = 1.0, jax.random.fold_in(stream_key, 6)
    for position, shards_of in cuts:
        draws = jnp.exp(jax.random.uniform(jax.random.fold_in(own, position), (shards_of,), jnp.float32, smallest / len(cuts), top_value / len(cuts)))
        loudness = loudness * jnp.repeat(draws, dims[position] // shards_of).reshape([-1 if axis == position else 1 for axis in range(len(dims))])
    return loudness


def noise(rng, extent, width, bound, shards=(), held_as=jnp.bfloat16):
    values = width * jax.random.normal(rng, extent, jnp.float32)
    if shards:
        values = values * levels(rng, extent, shards, -0.22, 0.18)
    return jnp.clip(values, -bound, bound).astype(held_as)


def setup_inputs(seed: int = 0) -> dict:
    arg_keys = jax.random.split(jax.random.key(seed), 9)
    query_stream = noise(arg_keys[0], (SEQ, D), 1.0, 6.0, ((0, 24), (1, 32)))
    key_stream = noise(arg_keys[1], (SEQ, D), 1.0, 6.0, ((0, 24), (1, 32)))
    value_stream = noise(arg_keys[2], (SEQ, D), 1.0, 6.0, ((0, 24), (1, 32)))
    short_filter = noise(arg_keys[3], (3, SHORT, D), SHORT ** -0.5, 2.0, ((2, 32),), jnp.float32)
    long_filter = noise(arg_keys[4], (GROUPS, LONG), LONG ** -0.5, 0.5, ((0, 32),))
    doc_start = draw_doc_start(jax.random.fold_in(arg_keys[8], 71), 0)
    out_weight = noise(arg_keys[6], (D, D), D ** -0.5, 0.0625, ((0, 32),))
    out_cotangent = noise(arg_keys[7], (SEQ, D), 1.0, 6.0, ((0, 768),))
    return {"query_stream": query_stream, "key_stream": key_stream, "value_stream": value_stream, "short_filter": short_filter, "long_filter": long_filter, "doc_start": doc_start, "out_weight": out_weight, "out_cotangent": out_cotangent}


def short_forward(stream, short_taps, doc_start):
    seq_len, all_width = stream.shape
    lead = short_taps.shape[0] - 1
    positions = jnp.arange(seq_len, dtype=jnp.int32)
    extended = jnp.concatenate([jnp.zeros((lead, all_width), jnp.float32), stream.astype(jnp.float32)])
    summed = jnp.zeros((seq_len, all_width), jnp.float32)
    for tap_index in range(lead + 1):
        usable = (positions - tap_index >= doc_start).astype(jnp.float32)[:, None]
        summed = summed + short_taps[tap_index][None, :] * extended[lead - tap_index: lead - tap_index + seq_len] * usable
    return summed


def short_backward(grads, short_taps, doc_start):
    seq_len, all_width = grads.shape
    lead = short_taps.shape[0] - 1
    positions = jnp.arange(seq_len, dtype=jnp.int32)
    grad_ext = jnp.concatenate([grads, jnp.zeros((lead, all_width), jnp.float32)])
    start_ext = jnp.concatenate([doc_start, jnp.full((lead,), seq_len, jnp.int32)])
    summed = jnp.zeros((seq_len, all_width), jnp.float32)
    for tap_index in range(lead + 1):
        usable = (positions >= start_ext[tap_index: tap_index + seq_len]).astype(jnp.float32)[:, None]
        summed = summed + short_taps[tap_index][None, :] * grad_ext[tap_index: tap_index + seq_len] * usable
    return summed


def long_forward(mixed, channel_taps, doc_start):
    seq_len, all_width = mixed.shape
    reach = channel_taps.shape[1] - 1
    positions = jnp.arange(seq_len, dtype=jnp.int32)
    padded = jnp.concatenate([jnp.zeros((reach, all_width), jnp.float32), mixed.astype(jnp.float32)])

    def add_tap(tap_index, running):
        tap_int = jnp.asarray(tap_index).astype(jnp.int32)
        source = lax.dynamic_slice_in_dim(padded, (reach - tap_int).astype(jnp.int32), seq_len, 0)
        usable = (positions - tap_int >= doc_start).astype(jnp.float32)[:, None]
        column = lax.dynamic_slice_in_dim(channel_taps, tap_int, 1, 1)[:, 0]
        return running + column[None, :] * source * usable

    return lax.fori_loop(0, reach + 1, add_tap, jnp.zeros((seq_len, all_width), jnp.float32))


def long_backward(grads, channel_taps, doc_start):
    seq_len, all_width = grads.shape
    reach = channel_taps.shape[1] - 1
    positions = jnp.arange(seq_len, dtype=jnp.int32)
    grad_ext = jnp.concatenate([grads.astype(jnp.float32), jnp.zeros((reach, all_width), jnp.float32)])
    start_ext = jnp.concatenate([doc_start, jnp.full((reach,), seq_len, jnp.int32)])

    def add_tap(tap_index, running):
        tap_int = jnp.asarray(tap_index).astype(jnp.int32)
        source = lax.dynamic_slice_in_dim(grad_ext, tap_int, seq_len, 0)
        later = lax.dynamic_slice_in_dim(start_ext, tap_int, seq_len, 0)
        usable = (positions >= later).astype(jnp.float32)[:, None]
        column = lax.dynamic_slice_in_dim(channel_taps, tap_int, 1, 1)[:, 0]
        return running + column[None, :] * source * usable

    return lax.fori_loop(0, reach + 1, add_tap, jnp.zeros((seq_len, all_width), jnp.float32))


def project(gated, out_weight):
    block_width = out_weight.shape[0] // N_TP

    def add_block(block_index, running):
        first_col = (jnp.asarray(block_index) * block_width).astype(jnp.int32)
        columns = lax.dynamic_slice_in_dim(gated, first_col, block_width, 1)
        weight_rows = lax.dynamic_slice_in_dim(out_weight, first_col, block_width, 0)
        partial_sum = jnp.dot(columns, weight_rows, preferred_element_type=jnp.float32)
        rounded = lax.optimization_barrier(partial_sum.astype(jnp.bfloat16))
        return running + rounded.astype(jnp.float32)

    start_value = jnp.zeros((gated.shape[0], out_weight.shape[1]), jnp.float32)
    return lax.fori_loop(0, N_TP, add_block, start_value)


def reference(query_stream, key_stream, value_stream, short_filter, long_filter, doc_start, out_weight, out_cotangent):
    query_short = short_forward(query_stream, short_filter[0], doc_start)
    key_short = short_forward(key_stream, short_filter[1], doc_start)
    value_short = short_forward(value_stream, short_filter[2], doc_start)
    mixed = (key_short * value_short).astype(jnp.bfloat16)
    channel_taps = jnp.repeat(long_filter.astype(jnp.float32), GRP, axis=0)
    filtered = long_forward(mixed, channel_taps, doc_start)
    gated = (query_short * filtered).astype(jnp.bfloat16)
    projected = project(gated, out_weight).astype(jnp.bfloat16)
    grad_gated = lax.dot_general(out_cotangent, out_weight, (((1,), (1,)), ((), ())), preferred_element_type=jnp.float32)
    grad_query = grad_gated * filtered
    grad_filtered = (grad_gated * query_short).astype(jnp.bfloat16)
    grad_mixed = long_backward(grad_filtered, channel_taps, doc_start)
    grad_key = grad_mixed * value_short
    grad_value = grad_mixed * key_short
    stream_grads = jnp.stack([
        short_backward(grad_query, short_filter[0], doc_start),
        short_backward(grad_key, short_filter[1], doc_start),
        short_backward(grad_value, short_filter[2], doc_start),
    ]).astype(jnp.bfloat16)
    return projected, stream_grads
```

```python
import jax
import jax.numpy as jnp
from jax import lax
from jax.sharding import PartitionSpec as P


def shifted(value, axis, steps):
    count = lax.axis_size(axis)
    first, last = (max(0, -steps), min(count, count - steps))
    return lax.ppermute(value, axis, [(source, source + steps) for source in range(first, last)])


def short_conv(extended, short_taps, positions, starts):
    lead = short_taps.shape[0] - 1
    length = positions.shape[0]
    summed = jnp.zeros((length, extended.shape[1]), jnp.float32)
    for tap_index in range(lead + 1):
        usable = (positions - tap_index >= starts).astype(jnp.float32)[:, None]
        source = extended[lead - tap_index : lead - tap_index + length].astype(jnp.float32)
        summed = summed + short_taps[tap_index][None, :] * source * usable
    return summed


def short_back(grads, short_taps, positions, starts):
    lead = short_taps.shape[0] - 1
    summed = jnp.zeros((grads.shape[0] + lead, grads.shape[1]), jnp.float32)
    for tap_index in range(lead + 1):
        usable = (positions - tap_index >= starts).astype(jnp.float32)[:, None]
        contrib = short_taps[tap_index][None, :] * grads * usable
        summed = summed + jnp.pad(contrib, ((lead - tap_index, tap_index), (0, 0)))
    return summed


def skew_table(filters):
    groups, taps = filters.shape
    head = jnp.concatenate(
        [
            jnp.zeros((groups, 1), filters.dtype),
            filters[:, ::-1],
            jnp.zeros((groups, taps), filters.dtype),
        ],
        axis=1,
    )
    tiled = jnp.tile(head, (1, taps))[:, : taps * 2 * taps]
    return tiled.reshape(groups, taps, 2 * taps)


def window_blocks(padded, block_rows):
    block_count = (padded.shape[0] - block_rows) // block_rows
    leading = padded[: block_count * block_rows].reshape(block_count, block_rows, -1)
    trailing = padded[block_rows:].reshape(block_count, block_rows, -1)
    return jnp.concatenate([leading, trailing], axis=1)


RING = 8
SHARE = 4


def tp_move(value, dy=0, flip_x=0, flip_core=0):
    pairs = []
    for source in range(RING * SHARE):
        ring_pos, side, core = (source // SHARE, source // 2 % 2, source % 2)
        target = (ring_pos + dy) % RING * SHARE + (side ^ flip_x) * 2 + (core ^ flip_core)
        pairs.append((source, target))
    return lax.ppermute(value, "tp", pairs)


def turn(blocks, steps):
    return lax.dynamic_slice_in_dim(jnp.concatenate([blocks, blocks]), steps, RING, 0)


def flips(blocks, side, core):
    blocks = jnp.where(side == 1, blocks[:, ::-1], blocks)
    return jnp.where(core == 1, blocks[:, :, ::-1], blocks)


def gather_cotangent(own):
    base = jnp.concatenate([own, tp_move(own, flip_x=1)])
    rows = own.shape[0]
    right, left = ([base], [base])
    for _ in range(3):
        right.append(tp_move(right[-1], dy=1))
        left.append(tp_move(left[-1], dy=-1))
    far = [tp_move(right[3][:rows], dy=1), tp_move(left[3][rows:], dy=-1)]
    return jnp.concatenate([base, *left[1:], *far, *right[:0:-1]])


def scatter_sum(parts):
    rows, width = parts.shape[2:]
    wide = parts.astype(jnp.float32)
    right = tp_move(parts[4, 0], dy=1)
    left = tp_move(parts[4, 1], dy=-1)
    none = jnp.zeros((1, rows, width), jnp.float32)
    right = jnp.concatenate([right[None].astype(jnp.float32), none])
    left = jnp.concatenate([none, left[None].astype(jnp.float32)])
    for step in (3, 2, 1):
        right = tp_move((wide[step] + right).astype(jnp.bfloat16), dy=1).astype(jnp.float32)
        left = tp_move((wide[RING - step] + left).astype(jnp.bfloat16), dy=-1).astype(jnp.float32)
    total = wide[0] + right + left
    other = tp_move(total[1].astype(jnp.bfloat16), flip_x=1)
    return (total[0] + other.astype(jnp.float32)).astype(jnp.bfloat16)


def body(
    query_stream,
    key_stream,
    value_stream,
    short_filter,
    long_filter,
    doc_start,
    out_weight,
    out_cotangent,
):
    tok_rows, channels = query_stream.shape
    block_rows = long_filter.shape[1]
    block_count = tok_rows // block_rows
    groups = long_filter.shape[0]
    lead = short_filter.shape[1] - 1
    reach = block_rows - 1
    shard_start = lax.axis_index("ctx") * tok_rows
    positions = shard_start + jnp.arange(tok_rows, dtype=jnp.int32)
    member = lax.axis_index("tp")
    ring_pos, side, core = (member // SHARE, member // 2 % 2, member % 2)
    gathered = gather_cotangent(out_cotangent)
    rim = reach + lead
    rim_rows = jnp.concatenate(
        [key_stream[-rim:], value_stream[-rim:], query_stream[-lead:]], axis=0
    )
    before = shifted(rim_rows, "ctx", 1)
    long_positions = shard_start - reach + jnp.arange(tok_rows + reach, dtype=jnp.int32)
    long_starts = jnp.concatenate([jnp.broadcast_to(doc_start[:1], (reach,)), doc_start])
    key_all = short_conv(
        jnp.concatenate([before[:rim], key_stream]), short_filter[1], long_positions, long_starts
    )
    value_all = short_conv(
        jnp.concatenate([before[rim : 2 * rim], value_stream]),
        short_filter[2],
        long_positions,
        long_starts,
    )
    mixed = (key_all * value_all).astype(jnp.bfloat16)
    key_short, value_short = (key_all[reach:], value_all[reach:])
    padded = jnp.concatenate([jnp.zeros((1, channels), jnp.bfloat16), mixed])
    query_short = short_conv(
        jnp.concatenate([before[2 * rim :], query_stream]), short_filter[0], positions, doc_start
    )
    columns = jnp.arange(2 * block_rows, dtype=jnp.int32)[None, None, :]
    block_base = (jnp.arange(block_count, dtype=jnp.int32) * block_rows)[:, None, None]
    source_pos = shard_start + block_base + columns - block_rows
    allowed = (source_pos >= doc_start.reshape(block_count, block_rows)[:, :, None]).astype(
        jnp.bfloat16
    )
    masked = skew_table(long_filter)[None] * allowed[:, None]
    windows = window_blocks(padded, block_rows).reshape(
        block_count, 2 * block_rows, groups, channels // groups
    )
    filtered = jnp.einsum(
        "bgrc,bcgk->brgk", masked, windows, preferred_element_type=jnp.float32
    ).reshape(tok_rows, channels)
    gated = (query_short * filtered).astype(jnp.bfloat16)
    own_rows = tok_rows // (RING * SHARE)
    shape = (RING, 2, 2, own_rows, channels)
    ordered = flips(turn(gated.reshape(shape), ring_pos), side, core)
    half = (RING * 2 * own_rows, channels)
    away = jnp.dot(
        ordered[:, :, 1].reshape(half), out_weight, preferred_element_type=jnp.float32
    ).astype(jnp.bfloat16)
    received = tp_move(away, flip_core=1)
    here = jnp.dot(ordered[:, :, 0].reshape(half), out_weight, preferred_element_type=jnp.float32)
    parts = (here + received.astype(jnp.float32)).astype(jnp.bfloat16)
    projected = scatter_sum(parts.reshape(RING, 2, own_rows, -1))
    dims = (((1,), (1,)), ((), ()))
    grad_here = lax.dot_general(gathered, out_weight, dims, preferred_element_type=jnp.float32)
    sibling = tp_move(gathered, flip_core=1)
    grad_there = lax.dot_general(sibling, out_weight, dims, preferred_element_type=jnp.float32)
    quads = (RING, 2, own_rows, channels)
    both = jnp.stack([grad_here.reshape(quads), grad_there.reshape(quads)], axis=2)
    grad_gated = turn(flips(both, side, core), (RING - ring_pos) % RING)
    grad_gated = grad_gated.reshape(tok_rows, channels)
    grad_query = grad_gated * filtered
    grad_filtered = (grad_gated * query_short).astype(jnp.bfloat16)
    grad_blocks = grad_filtered.reshape(block_count, block_rows, groups, channels // groups)
    spread = jnp.einsum("bgrc,brgk->bcgk", masked, grad_blocks, preferred_element_type=jnp.float32)
    spread = spread.reshape(block_count, 2 * block_rows, channels)
    grad_padded = jnp.pad(
        spread[:, :block_rows].reshape(tok_rows, channels), ((0, block_rows), (0, 0))
    )
    grad_padded = grad_padded + jnp.pad(
        spread[:, block_rows:].reshape(tok_rows, channels), ((block_rows, 0), (0, 0))
    )
    own_mixed = grad_padded[block_rows:]
    head_key = own_mixed[:lead] * value_short[:lead]
    head_value = own_mixed[:lead] * key_short[:lead]
    outgoing = [grad_padded[1:block_rows]]
    for head_grad, stream_index in ((grad_query[:lead], 0), (head_key, 1), (head_value, 2)):
        outgoing.append(
            short_back(head_grad, short_filter[stream_index], positions[:lead], doc_start[:lead])[
                :lead
            ]
        )
    from_next = shifted(jnp.concatenate(outgoing).astype(jnp.bfloat16), "ctx", -1).astype(
        jnp.float32
    )
    grad_mixed = own_mixed + jnp.pad(from_next[:reach], ((tok_rows - reach, 0), (0, 0)))
    grad_key = grad_mixed * value_short
    grad_value = grad_mixed * key_short
    results = []
    for stream_index, stream_grad in enumerate((grad_query, grad_key, grad_value)):
        local_part = short_back(stream_grad, short_filter[stream_index], positions, doc_start)[
            lead:
        ]
        incoming = from_next[reach + stream_index * lead : reach + (stream_index + 1) * lead]
        results.append(local_part + jnp.pad(incoming, ((tok_rows - lead, 0), (0, 0))))
    stream_grads = jnp.stack(results).astype(jnp.bfloat16)
    return (projected, stream_grads)


def solution(mesh):
    in_specs = (
        P("ctx", "tp"),
        P("ctx", "tp"),
        P("ctx", "tp"),
        P(None, None, "tp"),
        P("tp", None),
        P("ctx"),
        P("tp", None),
        P(("ctx", "tp"), None),
    )
    out_specs = (P(("ctx", "tp"), None), P(None, "ctx", "tp"))
    return jax.shard_map(body, mesh=mesh, in_specs=in_specs, out_specs=out_specs, check_vma=False)
```

```python
import jax
import jax.numpy as jnp
from jax import lax
from jax.sharding import PartitionSpec as P


def shifted(value, axis, steps):
    count = lax.axis_size(axis)
    first, last = (max(0, -steps), min(count, count - steps))
    return lax.ppermute(value, axis, [(source, source + steps) for source in range(first, last)])


def short_conv(extended, short_taps, positions, starts):
    lead = short_taps.shape[0] - 1
    length = positions.shape[0]
    summed = jnp.zeros((length, extended.shape[1]), jnp.float32)
    for tap_index in range(lead + 1):
        usable = (positions - tap_index >= starts).astype(jnp.float32)[:, None]
        source = extended[lead - tap_index : lead - tap_index + length].astype(jnp.float32)
        summed = summed + short_taps[tap_index][None, :] * source * usable
    return summed


def short_back(grads, short_taps, positions, starts):
    lead = short_taps.shape[0] - 1
    summed = jnp.zeros((grads.shape[0] + lead, grads.shape[1]), jnp.float32)
    for tap_index in range(lead + 1):
        usable = (positions - tap_index >= starts).astype(jnp.float32)[:, None]
        contrib = short_taps[tap_index][None, :] * grads * usable
        summed = summed + jnp.pad(contrib, ((lead - tap_index, tap_index), (0, 0)))
    return summed


def skew_table(filters):
    groups, taps = filters.shape
    head = jnp.concatenate(
        [
            jnp.zeros((groups, 1), filters.dtype),
            filters[:, ::-1],
            jnp.zeros((groups, taps), filters.dtype),
        ],
        axis=1,
    )
    tiled = jnp.tile(head, (1, taps))[:, : taps * 2 * taps]
    return tiled.reshape(groups, taps, 2 * taps)


def window_blocks(padded, block_rows):
    block_count = (padded.shape[0] - block_rows) // block_rows
    leading = padded[: block_count * block_rows].reshape(block_count, block_rows, -1)
    trailing = padded[block_rows:].reshape(block_count, block_rows, -1)
    return jnp.concatenate([leading, trailing], axis=1)


RING = 8
SHARE = 4


def tp_move(value, dy=0, flip_x=0, flip_core=0):
    pairs = []
    for source in range(RING * SHARE):
        ring_pos, side, core = (source // SHARE, source // 2 % 2, source % 2)
        target = (ring_pos + dy) % RING * SHARE + (side ^ flip_x) * 2 + (core ^ flip_core)
        pairs.append((source, target))
    return lax.ppermute(value, "tp", pairs)


def meet(*values):
    return lax.optimization_barrier(values)


def both_ways(right, left):
    return (tp_move(right, dy=1), tp_move(left, dy=-1))


def widen(value):
    return value.astype(jnp.float32)


def join(block, arrived):
    return (widen(block) + widen(arrived)).astype(jnp.bfloat16)


def owners(rows, ring_pos, side, core):
    place = jnp.arange(rows * 4 * RING, dtype=jnp.int32)
    other, step = (place // (rows * 2 * RING), place // (rows * 2) % RING)
    far, row = (place // rows % 2, place % rows)
    return ((ring_pos + step) % RING * 4 + (far ^ side) * 2 + (other ^ core)) * rows + row


def arrivals(rows, ring_pos, side, core):
    token = jnp.arange(rows * 4 * RING, dtype=jnp.int32)
    block, row = (token // rows, token % rows)
    other, far = (block % 2 ^ core, block // 2 % 2 ^ side)
    step = (block // 4 - ring_pos) % RING
    step = jnp.where(step < RING // 2, step, step - RING)
    slot = jnp.where(step > 0, 2 * step, jnp.maximum(-2 * step - 1, 0))
    return ((other * RING + slot) * 2 + far) * rows + row


def body(
    query_stream,
    key_stream,
    value_stream,
    short_filter,
    long_filter,
    doc_start,
    out_weight,
    out_cotangent,
):
    tok_rows, channels = query_stream.shape
    block_rows = long_filter.shape[1]
    block_count = tok_rows // block_rows
    groups = long_filter.shape[0]
    lead = short_filter.shape[1] - 1
    reach = block_rows - 1
    shard_start = lax.axis_index("ctx") * tok_rows
    positions = shard_start + jnp.arange(tok_rows, dtype=jnp.int32)
    member = lax.axis_index("tp")
    ring_pos, side, core = (member // SHARE, member // 2 % 2, member % 2)
    own_rows = tok_rows // (RING * SHARE)
    cross = tp_move(out_cotangent, flip_x=1)
    rim = reach + lead
    rim_rows = jnp.concatenate(
        [key_stream[-rim:], value_stream[-rim:], query_stream[-lead:]], axis=0
    )
    before = shifted(rim_rows, "ctx", 1)
    columns = jnp.arange(2 * block_rows, dtype=jnp.int32)[None, None, :]
    block_base = (jnp.arange(block_count, dtype=jnp.int32) * block_rows)[:, None, None]
    source_pos = shard_start + block_base + columns - block_rows
    allowed = (source_pos >= doc_start.reshape(block_count, block_rows)[:, :, None]).astype(
        jnp.bfloat16
    )
    table = skew_table(long_filter)
    cross, table, allowed = meet(cross, table, allowed)
    masked = table[None] * allowed[:, None]
    base = jnp.concatenate([out_cotangent, cross])
    right1, left1 = both_ways(base, base)

    long_positions = shard_start - reach + jnp.arange(tok_rows + reach, dtype=jnp.int32)
    long_starts = jnp.concatenate([jnp.broadcast_to(doc_start[:1], (reach,)), doc_start])
    key_all = short_conv(
        jnp.concatenate([before[:rim], key_stream]), short_filter[1], long_positions, long_starts
    )
    value_all = short_conv(
        jnp.concatenate([before[rim : 2 * rim], value_stream]),
        short_filter[2],
        long_positions,
        long_starts,
    )
    mixed = (key_all * value_all).astype(jnp.bfloat16)
    key_short, value_short = (key_all[reach:], value_all[reach:])
    padded = jnp.concatenate([jnp.zeros((1, channels), jnp.bfloat16), mixed])
    query_short = short_conv(
        jnp.concatenate([before[2 * rim :], query_stream]), short_filter[0], positions, doc_start
    )
    right1, left1, padded, query_short = meet(right1, left1, padded, query_short)
    right2, left2 = both_ways(right1, left1)

    windows = window_blocks(padded, block_rows).reshape(
        block_count, 2 * block_rows, groups, channels // groups
    )
    filtered = jnp.einsum(
        "bgrc,bcgk->brgk", masked, windows, preferred_element_type=jnp.float32
    ).reshape(tok_rows, channels)
    gated = (query_short * filtered).astype(jnp.bfloat16)
    token = jnp.arange(tok_rows, dtype=jnp.int32)
    pick = owners(own_rows, ring_pos, side, core)[:, None] == token[None, :]
    ordered = jnp.dot(
        pick.astype(jnp.bfloat16), gated, preferred_element_type=jnp.float32
    ).astype(jnp.bfloat16)
    right2, left2, ordered = meet(right2, left2, ordered)
    right3, left3 = both_ways(right2, left2)

    half = tok_rows // 2
    away = jnp.dot(ordered[half:], out_weight, preferred_element_type=jnp.float32)
    received = tp_move(away.astype(jnp.bfloat16), flip_core=1)
    right3, left3, received = meet(right3, left3, received)
    right4, left4 = both_ways(right3[:own_rows], left3[own_rows:])

    here = jnp.dot(ordered[:half], out_weight, preferred_element_type=jnp.float32)
    parts = (here + widen(received)).astype(jnp.bfloat16)
    right4, left4, parts = meet(right4, left4, parts)
    parts = parts.reshape(RING, 2, own_rows, -1)
    right, left = both_ways(parts[4, 0], parts[4, 1])

    gathered = jnp.concatenate(
        [base, right1, left1, right2, left2, right3, left3, right4, left4]
    )
    right, left, gathered = meet(right, left, gathered)
    sibling = tp_move(gathered, flip_core=1)
    right = jnp.stack([join(parts[3, 0], right), parts[3, 1]])
    left = jnp.stack([parts[5, 0], join(parts[5, 1], left)])
    right, left = both_ways(right, left)

    dims = (((1,), (1,)), ((), ()))
    grad_here = lax.dot_general(gathered, out_weight, dims, preferred_element_type=jnp.float32)
    right, left, grad_here, sibling = meet(right, left, grad_here, sibling)
    right, left = both_ways(join(parts[2], right), join(parts[6], left))

    grad_there = lax.dot_general(sibling, out_weight, dims, preferred_element_type=jnp.float32)
    place = arrivals(own_rows, ring_pos, side, core)[:, None] == token[None, :]
    grad_gated = jnp.dot(
        place.astype(jnp.float32),
        jnp.concatenate([grad_here, grad_there]),
        precision=lax.Precision.HIGHEST,
        preferred_element_type=jnp.float32,
    )
    right, left, grad_gated = meet(right, left, grad_gated)
    right, left = both_ways(join(parts[1], right), join(parts[7], left))

    grad_query = grad_gated * filtered
    grad_filtered = (grad_gated * query_short).astype(jnp.bfloat16)
    grad_blocks = grad_filtered.reshape(block_count, block_rows, groups, channels // groups)
    spread = jnp.einsum("bgrc,brgk->bcgk", masked, grad_blocks, preferred_element_type=jnp.float32)
    spread = spread.reshape(block_count, 2 * block_rows, channels)
    grad_padded = jnp.pad(
        spread[:, :block_rows].reshape(tok_rows, channels), ((0, block_rows), (0, 0))
    )
    grad_padded = grad_padded + jnp.pad(
        spread[:, block_rows:].reshape(tok_rows, channels), ((block_rows, 0), (0, 0))
    )
    own_mixed = grad_padded[block_rows:]
    head_key = own_mixed[:lead] * value_short[:lead]
    head_value = own_mixed[:lead] * key_short[:lead]
    outgoing = [grad_padded[1:block_rows]]
    for head_grad, stream_index in ((grad_query[:lead], 0), (head_key, 1), (head_value, 2)):
        outgoing.append(
            short_back(head_grad, short_filter[stream_index], positions[:lead], doc_start[:lead])[
                :lead
            ]
        )
    outgoing = jnp.concatenate(outgoing).astype(jnp.bfloat16)
    right, left, outgoing = meet(right, left, outgoing)
    from_next = widen(shifted(outgoing, "ctx", -1))
    total = widen(parts[0]) + widen(right) + widen(left)
    partner = tp_move(total[1].astype(jnp.bfloat16), flip_x=1)

    grad_mixed = own_mixed + jnp.pad(from_next[:reach], ((tok_rows - reach, 0), (0, 0)))
    grad_key = grad_mixed * value_short
    grad_value = grad_mixed * key_short
    results = []
    for stream_index, stream_grad in enumerate((grad_query, grad_key, grad_value)):
        local_part = short_back(stream_grad, short_filter[stream_index], positions, doc_start)[
            lead:
        ]
        incoming = from_next[reach + stream_index * lead : reach + (stream_index + 1) * lead]
        results.append(local_part + jnp.pad(incoming, ((tok_rows - lead, 0), (0, 0))))
    stream_grads = jnp.stack(results).astype(jnp.bfloat16)
    projected = (total[0] + widen(partner)).astype(jnp.bfloat16)
    return (projected, stream_grads)


def solution(mesh):
    in_specs = (
        P("ctx", "tp"),
        P("ctx", "tp"),
        P("ctx", "tp"),
        P(None, None, "tp"),
        P("tp", None),
        P("ctx"),
        P("tp", None),
        P(("ctx", "tp"), None),
    )
    out_specs = (P(("ctx", "tp"), None), P(None, "ctx", "tp"))
    return jax.shard_map(body, mesh=mesh, in_specs=in_specs, out_specs=out_specs, check_vma=False)
```

```python
import jax
import jax.numpy as jnp
from jax import lax
from jax.experimental import pallas as pl
from jax.experimental.pallas import tpu as pltpu
from jax.sharding import PartitionSpec as P


def shifted(value, axis, steps):
    count = lax.axis_size(axis)
    first, last = (max(0, -steps), min(count, count - steps))
    return lax.ppermute(value, axis, [(source, source + steps) for source in range(first, last)])


TAPS = 7
LONG = 128
ROWS = 256
WIDTH = 256
GROUPS = 16
RIM = 144
STRIP = 64


def tap_sum(source, reach, taps, stream, first, count, step):
    total = jnp.zeros((count, WIDTH), jnp.float32)
    for tap in range(TAPS):
        at = first + step * tap
        limits = reach[first : first + count] if step < 0 else reach[at : at + count]
        weighted = taps[stream, tap : tap + 1, :] * source[at : at + count, :]
        total = total + jnp.where(limits >= tap, weighted, 0.0)
    return total


def skewed(table, group):
    line = jnp.broadcast_to(table[group : group + 1, :], (LONG, 2 * LONG))
    return pltpu.roll(line, 0, 1, stride=1, stride_axis=0)


def lane_group():
    return lax.broadcasted_iota(jnp.int32, (LONG, WIDTH), 1) // (WIDTH // GROUPS)


def forward_kernel(
    rim, query, key, value, taps, table, spans, query_out, key_out, value_out, filtered, gated,
    query_all, key_all, value_all, reach, mixed,
):
    key_all[:RIM] = rim[:RIM].astype(jnp.float32)
    value_all[:RIM] = rim[RIM : 2 * RIM].astype(jnp.float32)
    query_all[:16] = rim[2 * RIM :].astype(jnp.float32)
    key_all[RIM:] = key[...].astype(jnp.float32)
    value_all[RIM:] = value[...].astype(jnp.float32)
    query_all[16:] = query[...].astype(jnp.float32)
    reach[:16] = jnp.full((16, WIDTH), -1, jnp.int32)
    reach[16:] = jnp.broadcast_to(spans[...], (ROWS + LONG, WIDTH))
    for top in range(0, ROWS + LONG, STRIP):
        key_strip = tap_sum(key_all, reach, taps, 1, top + 16, STRIP, -1)
        value_strip = tap_sum(value_all, reach, taps, 2, top + 16, STRIP, -1)
        mixed[top : top + STRIP] = (key_strip * value_strip).astype(jnp.bfloat16)
        if top >= LONG:
            key_out[top - LONG : top - LONG + STRIP] = key_strip
            value_out[top - LONG : top - LONG + STRIP] = value_strip
    reach[:ROWS] = reach[RIM : RIM + ROWS]
    for top in range(0, ROWS, STRIP):
        strip = jnp.zeros((STRIP, WIDTH), jnp.float32)
        for tap in range(TAPS):
            weighted = taps[0, tap : tap + 1, :] * query_all[top + 16 - tap : top + 16 - tap + STRIP]
            strip = strip + jnp.where(reach[top : top + STRIP] >= tap, weighted, 0.0)
        query_out[top : top + STRIP] = strip
    lanes = lane_group()
    column = lax.broadcasted_iota(jnp.int32, (LONG, 2 * LONG), 1)
    row = lax.broadcasted_iota(jnp.int32, (LONG, 2 * LONG), 0)
    allowed = [column - LONG - row >= -reach[:LONG], column - LONG - row >= -reach[LONG:ROWS]]
    for group in range(GROUPS):
        skew = skewed(table, group)
        for block in range(2):
            used = jnp.where(allowed[block], skew, 0.0).astype(jnp.bfloat16)
            window = mixed[block * LONG : block * LONG + 2 * LONG]
            found = jnp.dot(used, window, preferred_element_type=jnp.float32)
            rows = pl.ds(block * LONG, LONG)
            filtered[rows] = found if group == 0 else jnp.where(lanes == group, found, filtered[rows])
    gated[...] = (query_out[...] * filtered[...]).astype(jnp.bfloat16)


def backward_kernel(
    grad, filtered, query, key, value, taps, table, starts, spans, grad_query, own, leaving,
    pushed, small, limits,
):
    grad_query[...] = grad[...] * filtered[...]
    pushed[...] = (grad[...] * query[...]).astype(jnp.bfloat16)
    lanes = lane_group()
    row = lax.broadcasted_iota(jnp.int32, (LONG, 2 * LONG), 0)
    begins = jnp.broadcast_to(starts[...], (LONG, 2 * LONG))
    same = row >= begins
    later = (row + LONG >= begins)[:, LONG:]
    earlier = (row - LONG >= begins)[:, :LONG]
    before = jnp.zeros((LONG, WIDTH), jnp.float32)
    for group in range(GROUPS):
        skew = skewed(table, group)
        both = jnp.where(same, skew, 0.0).astype(jnp.bfloat16)
        found = jnp.dot(both, pushed[...], preferred_element_type=jnp.float32)
        own[:LONG] = found if group == 0 else jnp.where(lanes == group, found, own[:LONG])
        second = jnp.where(later, skew[:, :LONG], 0.0).astype(jnp.bfloat16)
        found = jnp.dot(second, pushed[LONG:], preferred_element_type=jnp.float32)
        own[LONG:] = found if group == 0 else jnp.where(lanes == group, found, own[LONG:])
        first = jnp.where(earlier, skew[:, LONG:], 0.0).astype(jnp.bfloat16)
        found = jnp.dot(first, pushed[:LONG], preferred_element_type=jnp.float32)
        before = jnp.where(lanes == group, found, before)
    leaving[:LONG] = before.astype(jnp.bfloat16)
    limits[:8] = jnp.full((8, WIDTH), -1, jnp.int32)
    limits[8:] = jnp.broadcast_to(spans[:8], (8, WIDTH))
    small[:8] = jnp.zeros((8, WIDTH), jnp.float32)
    heads = []
    for stream in range(3):
        if stream == 0:
            small[8:] = grad_query[:8]
        else:
            small[8:] = own[:8] * (value[:8] if stream == 1 else key[:8])
        total = jnp.zeros((8, WIDTH), jnp.float32)
        for tap in range(TAPS):
            weighted = taps[stream, tap : tap + 1, :] * small[tap : tap + 8]
            total = total + jnp.where(limits[tap : tap + 8] >= tap, weighted, 0.0)
        heads.append(total)
    heads.append(jnp.zeros((8, WIDTH), jnp.float32))
    leaving[LONG:] = jnp.concatenate(heads).astype(jnp.bfloat16)


def stream_kernel(grad_query, own, came, key, value, taps, spans, out, source, limits):
    limits[:ROWS] = jnp.broadcast_to(spans[...], (ROWS, WIDTH))
    limits[ROWS:] = jnp.full((8, WIDTH), -1, jnp.int32)
    source[ROWS:] = jnp.zeros((8, WIDTH), jnp.float32)
    tail = came[LONG:].astype(jnp.float32)
    for stream in range(3):
        if stream == 0:
            source[:ROWS] = grad_query[...]
        else:
            other = value if stream == 1 else key
            source[:LONG] = own[:LONG] * other[:LONG]
            source[LONG:ROWS] = (own[LONG:] + came[:LONG].astype(jnp.float32)) * other[LONG:]
        for top in range(0, ROWS, STRIP):
            strip = tap_sum(source, limits, taps, stream, top, STRIP, 1)
            if top + STRIP == ROWS:
                extra = jnp.zeros((STRIP - 8, WIDTH), jnp.float32)
                extra = jnp.concatenate([extra, tail[stream * 8 : stream * 8 + 8]])
                strip = strip + extra
            out[stream, top : top + STRIP] = strip.astype(jnp.bfloat16)


def wide(rows):
    return jax.ShapeDtypeStruct((rows, WIDTH), jnp.float32)


def narrow(*shape):
    return jax.ShapeDtypeStruct(shape, jnp.bfloat16)


def vmem(rows, kind):
    return pltpu.VMEM((rows, WIDTH), kind)


def run_forward(rim, query, key, value, taps, table, spans):
    return pl.pallas_call(
        forward_kernel,
        out_shape=[wide(ROWS)] * 4 + [narrow(ROWS, WIDTH)],
        scratch_shapes=[
            vmem(ROWS + 16, jnp.float32),
            vmem(ROWS + RIM, jnp.float32),
            vmem(ROWS + RIM, jnp.float32),
            vmem(ROWS + RIM, jnp.int32),
            vmem(ROWS + LONG, jnp.bfloat16),
        ],
    )(rim, query, key, value, taps, table, spans)


def run_backward(*arrays):
    return pl.pallas_call(
        backward_kernel,
        out_shape=[wide(ROWS), wide(ROWS), narrow(LONG + 32, WIDTH)],
        scratch_shapes=[
            vmem(ROWS, jnp.bfloat16),
            vmem(16, jnp.float32),
            vmem(16, jnp.int32),
        ],
    )(*arrays)


def run_streams(*arrays):
    return pl.pallas_call(
        stream_kernel,
        out_shape=narrow(3, ROWS, WIDTH),
        scratch_shapes=[vmem(ROWS + 8, jnp.float32), vmem(ROWS + 8, jnp.int32)],
    )(*arrays)


RING = 8
SHARE = 4


def tp_move(value, dy=0, flip_x=0, flip_core=0):
    pairs = []
    for source in range(RING * SHARE):
        ring_pos, side, core = (source // SHARE, source // 2 % 2, source % 2)
        target = (ring_pos + dy) % RING * SHARE + (side ^ flip_x) * 2 + (core ^ flip_core)
        pairs.append((source, target))
    return lax.ppermute(value, "tp", pairs)


def meet(*values):
    return lax.optimization_barrier(values)


def onward(value):
    pairs = []
    for source in range(RING * SHARE):
        step = 1 if source % 2 == 0 else RING - 1
        pairs.append((source, (source + step * SHARE) % (RING * SHARE)))
    return lax.ppermute(value, "tp", pairs)


def widen(value):
    return value.astype(jnp.float32)


def join(block, arrived):
    return (widen(block) + widen(arrived)).astype(jnp.bfloat16)


def owners(rows, ring_pos, side, core):
    place = jnp.arange(rows * 2 * RING, dtype=jnp.int32)
    place = jnp.where(place < 2 * rows, place, place + 2 * rows)
    step, other = (place // (4 * rows), place // (2 * rows) % 2)
    far, row = (place // rows % 2, place % rows)
    step = jnp.where(core == 0, step, RING - step)
    return ((ring_pos + step) % RING * 4 + (far ^ side) * 2 + (other ^ core)) * rows + row


def arrivals(rows, ring_pos, side, core):
    token = jnp.arange(rows * 4 * RING, dtype=jnp.int32)
    block, row = (token // rows, token % rows)
    other, far = (block % 2 ^ core, block // 2 % 2 ^ side)
    step = jnp.where(core == 0, ring_pos - block // 4, block // 4 - ring_pos) % RING
    mine = jnp.logical_or(step < 4, jnp.logical_and(step == 4, other == 0))
    here = (step * 4 + other * 2 + far) * rows + row
    there = ((RING - step) * 4 + (1 - other) * 2 + far) * rows + row + 18 * rows
    return jnp.where(mine, here, there)


def body(
    query_stream,
    key_stream,
    value_stream,
    short_filter,
    long_filter,
    doc_start,
    out_weight,
    out_cotangent,
):
    tok_rows = query_stream.shape[0]
    groups, taps = long_filter.shape
    member = lax.axis_index("tp")
    ring_pos, side, core = (member // SHARE, member // 2 % 2, member % 2)
    own_rows = tok_rows // (RING * SHARE)
    cross = tp_move(out_cotangent, flip_x=1)
    rim_rows = jnp.concatenate([key_stream[-RIM:], value_stream[-RIM:], query_stream[-16:]])
    before = shifted(rim_rows, "ctx", 1)
    begins = doc_start - lax.axis_index("ctx") * tok_rows
    spans = jnp.arange(-LONG, tok_rows, dtype=jnp.int32) - jnp.concatenate(
        [jnp.broadcast_to(begins[:1], (LONG,)), begins]
    )
    spans = spans[:, None]
    filters = widen(long_filter)
    behind = jnp.concatenate(
        [jnp.zeros((groups, 1)), filters[:, ::-1], jnp.zeros((groups, taps - 1))], axis=1
    )
    ahead = jnp.concatenate([filters, jnp.zeros((groups, taps))], axis=1)
    cross, behind, ahead, spans = meet(cross, behind, ahead, spans)
    pair = jnp.concatenate([out_cotangent, cross])
    quad = jnp.concatenate([pair, tp_move(pair, flip_core=1)])
    step1 = onward(quad)

    query_short, key_short, value_short, filtered, gated = run_forward(
        before, query_stream, key_stream, value_stream, short_filter, behind, spans
    )
    step1, gated = meet(step1, gated)
    step2 = onward(step1)

    token = jnp.arange(tok_rows, dtype=jnp.int32)
    half = tok_rows // 2
    mine = owners(own_rows, ring_pos, side, core)
    others = owners(own_rows, ring_pos, side, 1 - core)
    pick = jnp.concatenate([mine, others])[:, None] == token[None, :]
    ordered = jnp.dot(
        pick.astype(jnp.bfloat16), gated, preferred_element_type=jnp.float32
    ).astype(jnp.bfloat16)
    away = jnp.dot(ordered[half:], out_weight, preferred_element_type=jnp.float32)
    received = tp_move(away.astype(jnp.bfloat16), flip_core=1)
    step2, received, ordered = meet(step2, received, ordered)
    step3 = onward(step2)

    here = jnp.dot(ordered[:half], out_weight, preferred_element_type=jnp.float32)
    parts = (here + widen(received)).astype(jnp.bfloat16)
    step3, parts = meet(step3, parts)
    step4 = onward(step3[: 2 * own_rows])
    step4, parts = meet(step4, parts)
    unit = 2 * own_rows
    sums = onward(parts[7 * unit :])

    gathered = jnp.concatenate([quad, step1, step2, step3, step4])
    sums, gathered = meet(sums, gathered)
    sibling = tp_move(gathered, flip_core=1)
    sums = onward(
        jnp.concatenate([join(parts[5 * unit : 6 * unit], sums), parts[6 * unit : 7 * unit]])
    )

    dims = (((1,), (1,)), ((), ()))
    grad_here = lax.dot_general(gathered, out_weight, dims, preferred_element_type=jnp.float32)
    sums, grad_here, sibling = meet(sums, grad_here, sibling)
    sums = onward(join(parts[3 * unit : 5 * unit], sums))

    grad_there = lax.dot_general(sibling, out_weight, dims, preferred_element_type=jnp.float32)
    slots = jnp.arange(36 * own_rows, dtype=jnp.int32)
    place = arrivals(own_rows, ring_pos, side, core)[:, None] == slots[None, :]
    grad_gated = jnp.dot(
        place.astype(jnp.float32),
        jnp.concatenate([grad_here, grad_there]),
        precision=lax.Precision.HIGHEST,
        preferred_element_type=jnp.float32,
    )
    grad_query, own_mixed, outgoing = run_backward(
        grad_gated,
        filtered,
        query_short,
        key_short,
        value_short,
        short_filter,
        ahead,
        begins[None],
        spans[LONG:],
    )
    sums, outgoing = meet(sums, outgoing)
    sums = onward(join(parts[unit : 3 * unit], sums))
    from_next = shifted(outgoing, "ctx", -1)
    sums, from_next = meet(sums, from_next)
    crossed = tp_move(sums[unit:], flip_core=1)
    total = widen(parts[:unit]) + widen(sums[:unit]) + widen(crossed)
    partner = tp_move(total[own_rows:].astype(jnp.bfloat16), flip_x=1)

    stream_grads = run_streams(
        grad_query, own_mixed, from_next, key_short, value_short, short_filter, spans[LONG:]
    )
    projected = (total[:own_rows] + widen(partner)).astype(jnp.bfloat16)
    return (projected, stream_grads)


def solution(mesh):
    in_specs = (
        P("ctx", "tp"),
        P("ctx", "tp"),
        P("ctx", "tp"),
        P(None, None, "tp"),
        P("tp", None),
        P("ctx"),
        P("tp", None),
        P(("ctx", "tp"), None),
    )
    out_specs = (P(("ctx", "tp"), None), P(None, "ctx", "tp"))
    return jax.shard_map(body, mesh=mesh, in_specs=in_specs, out_specs=out_specs, check_vma=False)
```

```python
import jax
import jax.numpy as jnp
from jax import lax
from jax.experimental import pallas as pl
from jax.experimental.pallas import tpu as pltpu
from jax.sharding import PartitionSpec as P


def shifted(value, axis, steps):
    count = lax.axis_size(axis)
    first, last = (max(0, -steps), min(count, count - steps))
    return lax.ppermute(value, axis, [(source, source + steps) for source in range(first, last)])


TAPS = 7
LONG = 128
ROWS = 256
WIDTH = 256
GROUPS = 16
RIM = 144
STRIP = 64


def tap_sum(source, reach, taps, stream, first, count, step):
    total = jnp.zeros((count, WIDTH), jnp.float32)
    for tap in range(TAPS):
        at = first + step * tap
        limits = reach[first : first + count] if step < 0 else reach[at : at + count]
        weighted = taps[stream, tap : tap + 1, :] * source[at : at + count, :]
        total = total + jnp.where(limits >= tap, weighted, 0.0)
    return total


def skewed(table, group):
    line = jnp.broadcast_to(table[group : group + 1, :], (LONG, 2 * LONG))
    return pltpu.roll(line, 0, 1, stride=1, stride_axis=0)


def lane_group():
    return lax.broadcasted_iota(jnp.int32, (LONG, WIDTH), 1) // (WIDTH // GROUPS)


def forward_kernel(
    rim, query, key, value, taps, filters, begins, query_out, key_out, value_out, filtered, gated,
    spans, query_all, key_all, value_all, reach, mixed,
):
    starts = jnp.broadcast_to(begins[...].astype(jnp.float32), (ROWS, WIDTH)).T
    line = lax.broadcasted_iota(jnp.int32, (ROWS, WIDTH), 0)
    spans[...] = line - starts.astype(jnp.int32)
    first = jnp.broadcast_to(spans[:1], (LONG, WIDTH))
    flip = lax.broadcasted_iota(jnp.int32, (LONG, 2 * LONG), 0)
    flip = flip + lax.broadcasted_iota(jnp.int32, (LONG, 2 * LONG), 1) == LONG
    table = jnp.dot(filters[...], flip.astype(jnp.bfloat16), preferred_element_type=jnp.float32)
    key_all[:RIM] = rim[:RIM].astype(jnp.float32)
    value_all[:RIM] = rim[RIM : 2 * RIM].astype(jnp.float32)
    query_all[:16] = rim[2 * RIM :].astype(jnp.float32)
    key_all[RIM:] = key[...].astype(jnp.float32)
    value_all[RIM:] = value[...].astype(jnp.float32)
    query_all[16:] = query[...].astype(jnp.float32)
    reach[:16] = jnp.full((16, WIDTH), -1, jnp.int32)
    reach[16:RIM] = first + line[:LONG] - LONG
    reach[RIM:] = spans[...]
    for top in range(0, ROWS + LONG, STRIP):
        key_strip = tap_sum(key_all, reach, taps, 1, top + 16, STRIP, -1)
        value_strip = tap_sum(value_all, reach, taps, 2, top + 16, STRIP, -1)
        mixed[top : top + STRIP] = (key_strip * value_strip).astype(jnp.bfloat16)
        if top >= LONG:
            key_out[top - LONG : top - LONG + STRIP] = key_strip
            value_out[top - LONG : top - LONG + STRIP] = value_strip
    for top in range(0, ROWS, STRIP):
        strip = jnp.zeros((STRIP, WIDTH), jnp.float32)
        for tap in range(TAPS):
            weighted = taps[0, tap : tap + 1, :] * query_all[top + 16 - tap : top + 16 - tap + STRIP]
            strip = strip + jnp.where(spans[top : top + STRIP] >= tap, weighted, 0.0)
        query_out[top : top + STRIP] = strip
    lanes = lane_group()
    column = lax.broadcasted_iota(jnp.int32, (LONG, 2 * LONG), 1)
    row = lax.broadcasted_iota(jnp.int32, (LONG, 2 * LONG), 0)
    allowed = [column - LONG - row >= -spans[:LONG], column - LONG - row >= -spans[LONG:]]
    for group in range(GROUPS):
        skew = skewed(table, group)
        for block in range(2):
            used = jnp.where(allowed[block], skew, 0.0).astype(jnp.bfloat16)
            window = mixed[block * LONG : block * LONG + 2 * LONG]
            found = jnp.dot(used, window, preferred_element_type=jnp.float32)
            rows = pl.ds(block * LONG, LONG)
            filtered[rows] = found if group == 0 else jnp.where(lanes == group, found, filtered[rows])
    gated[...] = (query_out[...] * filtered[...]).astype(jnp.bfloat16)


def backward_kernel(
    grad, filtered, query, key, value, taps, filters, starts, spans, grad_query, own, leaving,
    pushed, small, limits,
):
    table = filters[...].astype(jnp.float32)
    table = jnp.concatenate([table, jnp.zeros((GROUPS, LONG), jnp.float32)], axis=1)
    grad_query[...] = grad[...] * filtered[...]
    pushed[...] = (grad[...] * query[...]).astype(jnp.bfloat16)
    lanes = lane_group()
    row = lax.broadcasted_iota(jnp.int32, (LONG, 2 * LONG), 0)
    begins = jnp.broadcast_to(starts[...], (LONG, 2 * LONG))
    same = row >= begins
    later = (row + LONG >= begins)[:, LONG:]
    earlier = (row - LONG >= begins)[:, :LONG]
    before = jnp.zeros((LONG, WIDTH), jnp.float32)
    for group in range(GROUPS):
        skew = skewed(table, group)
        both = jnp.where(same, skew, 0.0).astype(jnp.bfloat16)
        found = jnp.dot(both, pushed[...], preferred_element_type=jnp.float32)
        own[:LONG] = found if group == 0 else jnp.where(lanes == group, found, own[:LONG])
        second = jnp.where(later, skew[:, :LONG], 0.0).astype(jnp.bfloat16)
        found = jnp.dot(second, pushed[LONG:], preferred_element_type=jnp.float32)
        own[LONG:] = found if group == 0 else jnp.where(lanes == group, found, own[LONG:])
        first = jnp.where(earlier, skew[:, LONG:], 0.0).astype(jnp.bfloat16)
        found = jnp.dot(first, pushed[:LONG], preferred_element_type=jnp.float32)
        before = jnp.where(lanes == group, found, before)
    leaving[:LONG] = before.astype(jnp.bfloat16)
    limits[:8] = jnp.full((8, WIDTH), -1, jnp.int32)
    limits[8:] = spans[:8]
    small[:8] = jnp.zeros((8, WIDTH), jnp.float32)
    heads = []
    for stream in range(3):
        if stream == 0:
            small[8:] = grad_query[:8]
        else:
            small[8:] = own[:8] * (value[:8] if stream == 1 else key[:8])
        total = jnp.zeros((8, WIDTH), jnp.float32)
        for tap in range(TAPS):
            weighted = taps[stream, tap : tap + 1, :] * small[tap : tap + 8]
            total = total + jnp.where(limits[tap : tap + 8] >= tap, weighted, 0.0)
        heads.append(total)
    heads.append(jnp.zeros((8, WIDTH), jnp.float32))
    leaving[LONG:] = jnp.concatenate(heads).astype(jnp.bfloat16)


def rim_kernel(query, key, value, out):
    out[:RIM] = key[ROWS - RIM :]
    out[RIM : 2 * RIM] = value[ROWS - RIM :]
    out[2 * RIM :] = query[ROWS - 16 :]


def stream_kernel(grad_query, own, came, key, value, taps, spans, out, source, limits):
    limits[:ROWS] = spans[...]
    limits[ROWS:] = jnp.full((8, WIDTH), -1, jnp.int32)
    source[ROWS:] = jnp.zeros((8, WIDTH), jnp.float32)
    tail = came[LONG:].astype(jnp.float32)
    for stream in range(3):
        if stream == 0:
            source[:ROWS] = grad_query[...]
        else:
            other = value if stream == 1 else key
            source[:LONG] = own[:LONG] * other[:LONG]
            source[LONG:ROWS] = (own[LONG:] + came[:LONG].astype(jnp.float32)) * other[LONG:]
        for top in range(0, ROWS, STRIP):
            strip = tap_sum(source, limits, taps, stream, top, STRIP, 1)
            if top + STRIP == ROWS:
                extra = jnp.zeros((STRIP - 8, WIDTH), jnp.float32)
                extra = jnp.concatenate([extra, tail[stream * 8 : stream * 8 + 8]])
                strip = strip + extra
            out[stream, top : top + STRIP] = strip.astype(jnp.bfloat16)


def wide(rows):
    return jax.ShapeDtypeStruct((rows, WIDTH), jnp.float32)


def narrow(*shape):
    return jax.ShapeDtypeStruct(shape, jnp.bfloat16)


def vmem(rows, kind):
    return pltpu.VMEM((rows, WIDTH), kind)


def run_rim(*streams):
    return pl.pallas_call(rim_kernel, out_shape=narrow(2 * RIM + 16, WIDTH))(*streams)


def run_forward(*arrays):
    return pl.pallas_call(
        forward_kernel,
        out_shape=[wide(ROWS)] * 4
        + [narrow(ROWS, WIDTH), jax.ShapeDtypeStruct((ROWS, WIDTH), jnp.int32)],
        scratch_shapes=[
            vmem(ROWS + 16, jnp.float32),
            vmem(ROWS + RIM, jnp.float32),
            vmem(ROWS + RIM, jnp.float32),
            vmem(ROWS + RIM, jnp.int32),
            vmem(ROWS + LONG, jnp.bfloat16),
        ],
    )(*arrays)


def run_backward(*arrays):
    return pl.pallas_call(
        backward_kernel,
        out_shape=[wide(ROWS), wide(ROWS), narrow(LONG + 32, WIDTH)],
        scratch_shapes=[
            vmem(ROWS, jnp.bfloat16),
            vmem(16, jnp.float32),
            vmem(16, jnp.int32),
        ],
    )(*arrays)


def run_streams(*arrays):
    return pl.pallas_call(
        stream_kernel,
        out_shape=narrow(3, ROWS, WIDTH),
        scratch_shapes=[vmem(ROWS + 8, jnp.float32), vmem(ROWS + 8, jnp.int32)],
    )(*arrays)


RING = 8
SHARE = 4


def tp_move(value, dy=0, flip_x=0, flip_core=0):
    pairs = []
    for source in range(RING * SHARE):
        ring_pos, side, core = (source // SHARE, source // 2 % 2, source % 2)
        target = (ring_pos + dy) % RING * SHARE + (side ^ flip_x) * 2 + (core ^ flip_core)
        pairs.append((source, target))
    return lax.ppermute(value, "tp", pairs)


def meet(*values):
    return lax.optimization_barrier(values)


def reach_out(value, distance):
    pairs = []
    for source in range(RING * SHARE):
        step = distance if source % 2 == 0 else RING - distance
        pairs.append((source, (source + step * SHARE) % (RING * SHARE)))
    return lax.ppermute(value, "tp", pairs)


def widen(value):
    return value.astype(jnp.float32)


def join(block, arrived):
    return (widen(block) + widen(arrived)).astype(jnp.bfloat16)


def owners(rows, ring_pos, side, core):
    place = jnp.arange(rows * 2 * RING, dtype=jnp.int32)
    far, place = (place // (rows * RING), place % (rows * RING))
    place = jnp.where(place < rows, place, place + rows)
    step, other = (4 - place // (2 * rows), place // rows % 2)
    step = jnp.where(core == 0, step, RING - step)
    block = (ring_pos + step) % RING * 4 + (far ^ side) * 2 + (other ^ core)
    return block * rows + place % rows


def arrivals(rows, ring_pos, side, core):
    token = jnp.arange(rows * 4 * RING, dtype=jnp.int32)
    block, row = (token // rows, token % rows)
    other, far = (block % 2 ^ core, block // 2 % 2 ^ side)
    step = jnp.where(core == 0, ring_pos - block // 4, block // 4 - ring_pos) % RING
    sibling = jnp.where(step % 4 == 0, jnp.logical_and(other == 1, step + far > 0), step > 4)
    step = jnp.where(step > 4, RING - step, step)
    inner = jnp.where(step % 4 == 0, 0, jnp.where(sibling, 1 - other, other))
    place = jnp.where(
        step == 0, jnp.where(far == 1, 2, other), 3 + far * 7 + (step - 1) * 2 + inner
    )
    return (place + jnp.where(sibling, 17, 0)) * rows + row


def body(
    query_stream,
    key_stream,
    value_stream,
    short_filter,
    long_filter,
    doc_start,
    out_weight,
    out_cotangent,
):
    tok_rows = query_stream.shape[0]
    member = lax.axis_index("tp")
    ring_pos, side, core = (member // SHARE, member // 2 % 2, member % 2)
    own_rows = tok_rows // (RING * SHARE)
    mate = tp_move(out_cotangent, flip_core=1)
    rim_rows = run_rim(query_stream, key_stream, value_stream)
    before = shifted(rim_rows, "ctx", 1)
    begins = (doc_start - lax.axis_index("ctx") * tok_rows)[None]
    cross = tp_move(out_cotangent, flip_x=1)
    pair = jnp.concatenate([out_cotangent, mate])
    near = [reach_out(pair, 1), reach_out(pair, 2), reach_out(pair, 3)]
    near.append(reach_out(out_cotangent, 4))

    query_short, key_short, value_short, filtered, gated, spans = run_forward(
        before, query_stream, key_stream, value_stream, short_filter, long_filter, begins
    )
    token = jnp.arange(tok_rows, dtype=jnp.int32)
    half = tok_rows // 2
    mine = owners(own_rows, ring_pos, side, core)
    others = owners(own_rows, ring_pos, side, 1 - core)
    pick = jnp.concatenate([mine, others])[:, None] == token[None, :]
    ordered = jnp.dot(
        pick.astype(jnp.bfloat16), gated, preferred_element_type=jnp.float32
    ).astype(jnp.bfloat16)
    away = jnp.dot(ordered[half:], out_weight, preferred_element_type=jnp.float32)
    received = tp_move(away.astype(jnp.bfloat16), flip_core=1)
    here = jnp.dot(ordered[:half], out_weight, preferred_element_type=jnp.float32)
    parts = (here + widen(received)).astype(jnp.bfloat16)
    unit = own_rows
    bounds = [0, 3 * unit, 5 * unit, half // 2]
    inner = jnp.concatenate(near[:2])
    outer = jnp.concatenate(near[2:])
    inner_cross = tp_move(inner, flip_x=1)
    outer_cross = tp_move(outer, flip_x=1)
    leave = [parts[half // 2 + low : half // 2 + high] for low, high in zip(bounds, bounds[1:])]
    inner_cross, leave[0] = meet(inner_cross, leave[0])
    swapped = [tp_move(leave[0], flip_x=1)]
    outer_cross, leave[1] = meet(outer_cross, leave[1])
    swapped.append(tp_move(leave[1], flip_x=1))
    swapped[0], leave[2] = meet(swapped[0], leave[2])
    swapped.append(tp_move(leave[2], flip_x=1))
    gathered = jnp.concatenate(
        [pair, cross, inner, outer, inner_cross, outer_cross]
    )
    sibling = tp_move(gathered, flip_core=1)

    joined = [
        join(parts[low:high], arrived)
        for low, high, arrived in zip(bounds, bounds[1:], swapped)
    ]
    sums = [reach_out(joined[0][:unit], 4), reach_out(joined[0][unit:], 3)]
    sums += [reach_out(joined[1], 2), reach_out(joined[2][: 2 * unit], 1)]

    dims = (((1,), (1,)), ((), ()))
    grad_here = lax.dot_general(gathered, out_weight, dims, preferred_element_type=jnp.float32)

    grad_there = lax.dot_general(sibling, out_weight, dims, preferred_element_type=jnp.float32)
    slots = jnp.arange(34 * own_rows, dtype=jnp.int32)
    place = arrivals(own_rows, ring_pos, side, core)[:, None] == slots[None, :]
    grad_gated = jnp.dot(
        place.astype(jnp.float32),
        jnp.concatenate([grad_here, grad_there]),
        precision=lax.Precision.HIGHEST,
        preferred_element_type=jnp.float32,
    )
    grad_query, own_mixed, outgoing = run_backward(
        grad_gated,
        filtered,
        query_short,
        key_short,
        value_short,
        short_filter,
        long_filter,
        begins,
        spans,
    )
    from_next = shifted(outgoing, "ctx", -1)
    total = widen(sums[1]) + widen(sums[2]) + widen(sums[3])
    crossed = tp_move(total[unit:].astype(jnp.bfloat16), flip_core=1)
    total = total[:unit] + widen(sums[0]) + widen(joined[2][2 * unit :]) + widen(crossed)

    stream_grads = run_streams(
        grad_query, own_mixed, from_next, key_short, value_short, short_filter, spans
    )
    projected = total.astype(jnp.bfloat16)
    return (projected, stream_grads)


def solution(mesh):
    in_specs = (
        P("ctx", "tp"),
        P("ctx", "tp"),
        P("ctx", "tp"),
        P(None, None, "tp"),
        P("tp", None),
        P("ctx"),
        P("tp", None),
        P(("ctx", "tp"), None),
    )
    out_specs = (P(("ctx", "tp"), None), P(None, "ctx", "tp"))
    return jax.shard_map(body, mesh=mesh, in_specs=in_specs, out_specs=out_specs, check_vma=False)
```

```python
import jax
import jax.numpy as jnp
from jax import lax
from jax.experimental import pallas as pl
from jax.experimental.pallas import tpu as pltpu
from jax.sharding import PartitionSpec as P


def shifted(value, axis, steps):
    count = lax.axis_size(axis)
    first, last = (max(0, -steps), min(count, count - steps))
    return lax.ppermute(value, axis, [(source, source + steps) for source in range(first, last)])


TAPS = 7
LONG = 128
ROWS = 256
WIDTH = 256
GROUPS = 16
RIM = 144
STRIP = 64


def tap_sum(source, reach, taps, stream, first, count, step):
    total = jnp.zeros((count, WIDTH), jnp.float32)
    for tap in range(TAPS):
        at = first + step * tap
        limits = reach[first : first + count] if step < 0 else reach[at : at + count]
        weighted = taps[stream, tap : tap + 1, :] * source[at : at + count, :]
        total = total + jnp.where(limits >= tap, weighted, 0.0)
    return total


def skewed(table, group):
    line = jnp.broadcast_to(table[group : group + 1, :], (LONG, 2 * LONG))
    return pltpu.roll(line, 0, 1, stride=1, stride_axis=0)


def lane_group():
    return lax.broadcasted_iota(jnp.int32, (LONG, WIDTH), 1) // (WIDTH // GROUPS)


def forward_kernel(
    rim, query, key, value, taps, filters, begins, query_out, key_out, value_out, filtered, gated,
    spans, query_all, key_all, value_all, reach, mixed,
):
    starts = jnp.broadcast_to(begins[...].astype(jnp.float32), (ROWS, WIDTH)).T
    line = lax.broadcasted_iota(jnp.int32, (ROWS, WIDTH), 0)
    spans[...] = line - starts.astype(jnp.int32)
    first = jnp.broadcast_to(spans[:1], (LONG, WIDTH))
    flip = lax.broadcasted_iota(jnp.int32, (LONG, 2 * LONG), 0)
    flip = flip + lax.broadcasted_iota(jnp.int32, (LONG, 2 * LONG), 1) == LONG
    table = jnp.dot(filters[...], flip.astype(jnp.bfloat16), preferred_element_type=jnp.float32)
    key_all[:RIM] = rim[:RIM].astype(jnp.float32)
    value_all[:RIM] = rim[RIM : 2 * RIM].astype(jnp.float32)
    query_all[:16] = rim[2 * RIM :].astype(jnp.float32)
    key_all[RIM:] = key[...].astype(jnp.float32)
    value_all[RIM:] = value[...].astype(jnp.float32)
    query_all[16:] = query[...].astype(jnp.float32)
    reach[:16] = jnp.full((16, WIDTH), -1, jnp.int32)
    reach[16:RIM] = first + line[:LONG] - LONG
    reach[RIM:] = spans[...]
    for top in range(0, ROWS + LONG, STRIP):
        key_strip = tap_sum(key_all, reach, taps, 1, top + 16, STRIP, -1)
        value_strip = tap_sum(value_all, reach, taps, 2, top + 16, STRIP, -1)
        mixed[top : top + STRIP] = (key_strip * value_strip).astype(jnp.bfloat16)
        if top >= LONG:
            key_out[top - LONG : top - LONG + STRIP] = key_strip
            value_out[top - LONG : top - LONG + STRIP] = value_strip
    for top in range(0, ROWS, STRIP):
        strip = jnp.zeros((STRIP, WIDTH), jnp.float32)
        for tap in range(TAPS):
            weighted = taps[0, tap : tap + 1, :] * query_all[top + 16 - tap : top + 16 - tap + STRIP]
            strip = strip + jnp.where(spans[top : top + STRIP] >= tap, weighted, 0.0)
        query_out[top : top + STRIP] = strip
    lanes = lane_group()
    column = lax.broadcasted_iota(jnp.int32, (LONG, 2 * LONG), 1)
    row = lax.broadcasted_iota(jnp.int32, (LONG, 2 * LONG), 0)
    allowed = [column - LONG - row >= -spans[:LONG], column - LONG - row >= -spans[LONG:]]
    for group in range(GROUPS):
        skew = skewed(table, group)
        for block in range(2):
            used = jnp.where(allowed[block], skew, 0.0).astype(jnp.bfloat16)
            window = mixed[block * LONG : block * LONG + 2 * LONG]
            found = jnp.dot(used, window, preferred_element_type=jnp.float32)
            rows = pl.ds(block * LONG, LONG)
            filtered[rows] = found if group == 0 else jnp.where(lanes == group, found, filtered[rows])
    gated[...] = (query_out[...] * filtered[...]).astype(jnp.bfloat16)


def backward_kernel(
    grad, filtered, query, key, value, taps, filters, starts, spans, grad_query, own, leaving,
    pushed, small, limits,
):
    table = filters[...].astype(jnp.float32)
    table = jnp.concatenate([table, jnp.zeros((GROUPS, LONG), jnp.float32)], axis=1)
    grad_query[...] = grad[...] * filtered[...]
    pushed[...] = (grad[...] * query[...]).astype(jnp.bfloat16)
    lanes = lane_group()
    row = lax.broadcasted_iota(jnp.int32, (LONG, 2 * LONG), 0)
    begins = jnp.broadcast_to(starts[...], (LONG, 2 * LONG))
    same = row >= begins
    later = (row + LONG >= begins)[:, LONG:]
    earlier = (row - LONG >= begins)[:, :LONG]
    before = jnp.zeros((LONG, WIDTH), jnp.float32)
    for group in range(GROUPS):
        skew = skewed(table, group)
        both = jnp.where(same, skew, 0.0).astype(jnp.bfloat16)
        found = jnp.dot(both, pushed[...], preferred_element_type=jnp.float32)
        own[:LONG] = found if group == 0 else jnp.where(lanes == group, found, own[:LONG])
        second = jnp.where(later, skew[:, :LONG], 0.0).astype(jnp.bfloat16)
        found = jnp.dot(second, pushed[LONG:], preferred_element_type=jnp.float32)
        own[LONG:] = found if group == 0 else jnp.where(lanes == group, found, own[LONG:])
        first = jnp.where(earlier, skew[:, LONG:], 0.0).astype(jnp.bfloat16)
        found = jnp.dot(first, pushed[:LONG], preferred_element_type=jnp.float32)
        before = jnp.where(lanes == group, found, before)
    leaving[:LONG] = before.astype(jnp.bfloat16)
    limits[:8] = jnp.full((8, WIDTH), -1, jnp.int32)
    limits[8:] = spans[:8]
    small[:8] = jnp.zeros((8, WIDTH), jnp.float32)
    heads = []
    for stream in range(3):
        if stream == 0:
            small[8:] = grad_query[:8]
        else:
            small[8:] = own[:8] * (value[:8] if stream == 1 else key[:8])
        total = jnp.zeros((8, WIDTH), jnp.float32)
        for tap in range(TAPS):
            weighted = taps[stream, tap : tap + 1, :] * small[tap : tap + 8]
            total = total + jnp.where(limits[tap : tap + 8] >= tap, weighted, 0.0)
        heads.append(total)
    heads.append(jnp.zeros((8, WIDTH), jnp.float32))
    leaving[LONG:] = jnp.concatenate(heads).astype(jnp.bfloat16)


def rim_kernel(query, key, value, out):
    out[:RIM] = key[ROWS - RIM :]
    out[RIM : 2 * RIM] = value[ROWS - RIM :]
    out[2 * RIM :] = query[ROWS - 16 :]


def stream_kernel(grad_query, own, came, key, value, taps, spans, out, source, limits):
    limits[:ROWS] = spans[...]
    limits[ROWS:] = jnp.full((8, WIDTH), -1, jnp.int32)
    source[ROWS:] = jnp.zeros((8, WIDTH), jnp.float32)
    tail = came[LONG:].astype(jnp.float32)
    for stream in range(3):
        if stream == 0:
            source[:ROWS] = grad_query[...]
        else:
            other = value if stream == 1 else key
            source[:LONG] = own[:LONG] * other[:LONG]
            source[LONG:ROWS] = (own[LONG:] + came[:LONG].astype(jnp.float32)) * other[LONG:]
        for top in range(0, ROWS, STRIP):
            strip = tap_sum(source, limits, taps, stream, top, STRIP, 1)
            if top + STRIP == ROWS:
                extra = jnp.zeros((STRIP - 8, WIDTH), jnp.float32)
                extra = jnp.concatenate([extra, tail[stream * 8 : stream * 8 + 8]])
                strip = strip + extra
            out[stream, top : top + STRIP] = strip.astype(jnp.bfloat16)


def wide(rows):
    return jax.ShapeDtypeStruct((rows, WIDTH), jnp.float32)


def narrow(*shape):
    return jax.ShapeDtypeStruct(shape, jnp.bfloat16)


def vmem(rows, kind):
    return pltpu.VMEM((rows, WIDTH), kind)


def run_rim(*streams):
    return pl.pallas_call(rim_kernel, out_shape=narrow(2 * RIM + 16, WIDTH))(*streams)


def run_forward(*arrays):
    return pl.pallas_call(
        forward_kernel,
        out_shape=[wide(ROWS)] * 4
        + [narrow(ROWS, WIDTH), jax.ShapeDtypeStruct((ROWS, WIDTH), jnp.int32)],
        scratch_shapes=[
            vmem(ROWS + 16, jnp.float32),
            vmem(ROWS + RIM, jnp.float32),
            vmem(ROWS + RIM, jnp.float32),
            vmem(ROWS + RIM, jnp.int32),
            vmem(ROWS + LONG, jnp.bfloat16),
        ],
    )(*arrays)


def run_backward(*arrays):
    return pl.pallas_call(
        backward_kernel,
        out_shape=[wide(ROWS), wide(ROWS), narrow(LONG + 32, WIDTH)],
        scratch_shapes=[
            vmem(ROWS, jnp.bfloat16),
            vmem(16, jnp.float32),
            vmem(16, jnp.int32),
        ],
    )(*arrays)


def run_streams(*arrays):
    return pl.pallas_call(
        stream_kernel,
        out_shape=narrow(3, ROWS, WIDTH),
        scratch_shapes=[vmem(ROWS + 8, jnp.float32), vmem(ROWS + 8, jnp.int32)],
    )(*arrays)


RING = 8
SHARE = 4


def tp_move(value, dy=0, flip_x=0, flip_core=0):
    pairs = []
    for source in range(RING * SHARE):
        ring_pos, side, core = (source // SHARE, source // 2 % 2, source % 2)
        target = (ring_pos + dy) % RING * SHARE + (side ^ flip_x) * 2 + (core ^ flip_core)
        pairs.append((source, target))
    return lax.ppermute(value, "tp", pairs)


def meet(*values):
    return lax.optimization_barrier(values)


def onward(value):
    pairs = []
    for source in range(RING * SHARE):
        step = 1 if source % 2 == 0 else RING - 1
        pairs.append((source, (source + step * SHARE) % (RING * SHARE)))
    return lax.ppermute(value, "tp", pairs)


def widen(value):
    return value.astype(jnp.float32)


def join(block, arrived):
    return (widen(block) + widen(arrived)).astype(jnp.bfloat16)


def owners(rows, side, core):
    place = jnp.arange(rows * 2 * RING, dtype=jnp.int32)
    ring_pos, far = (place // (2 * rows), place // rows % 2)
    return ring_pos * 4 * rows + (far ^ side) * 2 * rows + core * rows + place % rows


def arrivals(rows, ring_pos, side, core):
    token = jnp.arange(rows * 4 * RING, dtype=jnp.int32)
    block, row = (token // rows, token % rows)
    other, far = (block % 2 ^ core, block // 2 % 2 ^ side)
    step = jnp.where(core == 0, ring_pos - block // 4, block // 4 - ring_pos) % RING
    mine = jnp.logical_or(step < 4, jnp.logical_and(step == 4, other == 0))
    here = (step * 4 + other * 2 + far) * rows + row
    there = ((RING - step) * 4 + (1 - other) * 2 + far) * rows + row + 18 * rows
    return jnp.where(mine, here, there)


def body(
    query_stream,
    key_stream,
    value_stream,
    short_filter,
    long_filter,
    doc_start,
    out_weight,
    out_cotangent,
):
    tok_rows = query_stream.shape[0]
    member = lax.axis_index("tp")
    ring_pos, side, core = (member // SHARE, member // 2 % 2, member % 2)
    own_rows = tok_rows // (RING * SHARE)
    rim_rows = run_rim(query_stream, key_stream, value_stream)
    before = shifted(rim_rows, "ctx", 1)
    begins = (doc_start - lax.axis_index("ctx") * tok_rows)[None]
    cross = tp_move(out_cotangent, flip_x=1)
    pair = jnp.concatenate([out_cotangent, cross])
    quad = jnp.concatenate([pair, tp_move(pair, flip_core=1)])
    step1 = onward(quad)

    query_short, key_short, value_short, filtered, gated, spans = run_forward(
        before, query_stream, key_stream, value_stream, short_filter, long_filter, begins
    )
    token = jnp.arange(tok_rows, dtype=jnp.int32)
    half = tok_rows // 2
    mine = owners(own_rows, side, core)
    others = owners(own_rows, side, 1 - core)
    pick = jnp.concatenate([mine, others])[:, None] == token[None, :]
    ordered = jnp.dot(
        pick.astype(jnp.bfloat16), gated, preferred_element_type=jnp.float32
    ).astype(jnp.bfloat16)
    away = jnp.dot(ordered[half:], out_weight, preferred_element_type=jnp.float32)
    received = tp_move(away.astype(jnp.bfloat16), flip_core=1)
    here = jnp.dot(ordered[:half], out_weight, preferred_element_type=jnp.float32)
    parts = (here + widen(received)).astype(jnp.bfloat16)
    step1, parts = meet(step1, parts)
    rings = [[place * SHARE + share for place in range(RING)] for share in range(SHARE)]
    sums = lax.psum_scatter(
        parts, "tp", scatter_dimension=0, axis_index_groups=rings, tiled=True
    )
    step2 = onward(step1)
    step3 = onward(step2)
    step4 = onward(step3[: 2 * own_rows])
    gathered = jnp.concatenate([quad, step1, step2, step3, step4])
    sibling = tp_move(gathered, flip_core=1)
    partner = tp_move(sums[own_rows:], flip_x=1)
    projected = join(sums[:own_rows], partner)

    dims = (((1,), (1,)), ((), ()))
    grad_here = lax.dot_general(gathered, out_weight, dims, preferred_element_type=jnp.float32)

    grad_there = lax.dot_general(sibling, out_weight, dims, preferred_element_type=jnp.float32)
    slots = jnp.arange(36 * own_rows, dtype=jnp.int32)
    place = arrivals(own_rows, ring_pos, side, core)[:, None] == slots[None, :]
    grad_gated = jnp.dot(
        place.astype(jnp.float32),
        jnp.concatenate([grad_here, grad_there]),
        precision=lax.Precision.HIGHEST,
        preferred_element_type=jnp.float32,
    )
    grad_query, own_mixed, outgoing = run_backward(
        grad_gated,
        filtered,
        query_short,
        key_short,
        value_short,
        short_filter,
        long_filter,
        begins,
        spans,
    )
    from_next = shifted(outgoing, "ctx", -1)
    stream_grads = run_streams(
        grad_query, own_mixed, from_next, key_short, value_short, short_filter, spans
    )
    return (projected, stream_grads)


def solution(mesh):
    in_specs = (
        P("ctx", "tp"),
        P("ctx", "tp"),
        P("ctx", "tp"),
        P(None, None, "tp"),
        P("tp", None),
        P("ctx"),
        P("tp", None),
        P(("ctx", "tp"), None),
    )
    out_specs = (P(("ctx", "tp"), None), P(None, "ctx", "tp"))
    return jax.shard_map(body, mesh=mesh, in_specs=in_specs, out_specs=out_specs, check_vma=False)
```

```python
import jax
import jax.numpy as jnp
from jax import lax
from jax.experimental import pallas as pl
from jax.experimental.pallas import tpu as pltpu
from jax.sharding import PartitionSpec as P


def shifted(value, axis, steps):
    count = lax.axis_size(axis)
    first, last = (max(0, -steps), min(count, count - steps))
    return lax.ppermute(value, axis, [(source, source + steps) for source in range(first, last)])


TAPS = 7
LONG = 128
ROWS = 256
WIDTH = 256
GROUPS = 16
RIM = 144
STRIP = 64


def tap_sum(source, reach, taps, stream, first, count, step):
    total = jnp.zeros((count, WIDTH), jnp.float32)
    for tap in range(TAPS):
        at = first + step * tap
        limits = reach[first : first + count] if step < 0 else reach[at : at + count]
        weighted = taps[stream, tap : tap + 1, :] * source[at : at + count, :]
        total = total + jnp.where(limits >= tap, weighted, 0.0)
    return total


def skewed(table, group):
    line = jnp.broadcast_to(table[group : group + 1, :], (LONG, 2 * LONG))
    return pltpu.roll(line, 0, 1, stride=1, stride_axis=0)


def lane_group():
    return lax.broadcasted_iota(jnp.int32, (LONG, WIDTH), 1) // (WIDTH // GROUPS)


def forward_kernel(
    rim, query, key, value, taps, filters, begins, query_out, key_out, value_out, filtered, gated,
    spans, query_all, key_all, value_all, reach, mixed,
):
    starts = jnp.broadcast_to(begins[...].astype(jnp.float32), (ROWS, WIDTH)).T
    line = lax.broadcasted_iota(jnp.int32, (ROWS, WIDTH), 0)
    spans[...] = line - starts.astype(jnp.int32)
    first = jnp.broadcast_to(spans[:1], (LONG, WIDTH))
    flip = lax.broadcasted_iota(jnp.int32, (LONG, 2 * LONG), 0)
    flip = flip + lax.broadcasted_iota(jnp.int32, (LONG, 2 * LONG), 1) == LONG
    table = jnp.dot(filters[...], flip.astype(jnp.bfloat16), preferred_element_type=jnp.float32)
    key_all[:RIM] = rim[:RIM].astype(jnp.float32)
    value_all[:RIM] = rim[RIM : 2 * RIM].astype(jnp.float32)
    query_all[:16] = rim[2 * RIM :].astype(jnp.float32)
    key_all[RIM:] = key[...].astype(jnp.float32)
    value_all[RIM:] = value[...].astype(jnp.float32)
    query_all[16:] = query[...].astype(jnp.float32)
    reach[:16] = jnp.full((16, WIDTH), -1, jnp.int32)
    reach[16:RIM] = first + line[:LONG] - LONG
    reach[RIM:] = spans[...]
    for top in range(0, ROWS + LONG, STRIP):
        key_strip = tap_sum(key_all, reach, taps, 1, top + 16, STRIP, -1)
        value_strip = tap_sum(value_all, reach, taps, 2, top + 16, STRIP, -1)
        mixed[top : top + STRIP] = (key_strip * value_strip).astype(jnp.bfloat16)
        if top >= LONG:
            key_out[top - LONG : top - LONG + STRIP] = key_strip
            value_out[top - LONG : top - LONG + STRIP] = value_strip
    for top in range(0, ROWS, STRIP):
        strip = jnp.zeros((STRIP, WIDTH), jnp.float32)
        for tap in range(TAPS):
            weighted = taps[0, tap : tap + 1, :] * query_all[top + 16 - tap : top + 16 - tap + STRIP]
            strip = strip + jnp.where(spans[top : top + STRIP] >= tap, weighted, 0.0)
        query_out[top : top + STRIP] = strip
    lanes = lane_group()
    column = lax.broadcasted_iota(jnp.int32, (LONG, 2 * LONG), 1)
    row = lax.broadcasted_iota(jnp.int32, (LONG, 2 * LONG), 0)
    allowed = [column - LONG - row >= -spans[:LONG], column - LONG - row >= -spans[LONG:]]
    for group in range(GROUPS):
        skew = skewed(table, group)
        for block in range(2):
            used = jnp.where(allowed[block], skew, 0.0).astype(jnp.bfloat16)
            window = mixed[block * LONG : block * LONG + 2 * LONG]
            found = jnp.dot(used, window, preferred_element_type=jnp.float32)
            rows = pl.ds(block * LONG, LONG)
            filtered[rows] = found if group == 0 else jnp.where(lanes == group, found, filtered[rows])
    gated[...] = (query_out[...] * filtered[...]).astype(jnp.bfloat16)


def backward_kernel(
    grad, filtered, query, key, value, taps, filters, starts, spans, grad_query, own, leaving,
    pushed, small, limits,
):
    table = filters[...].astype(jnp.float32)
    table = jnp.concatenate([table, jnp.zeros((GROUPS, LONG), jnp.float32)], axis=1)
    grad_query[...] = grad[...] * filtered[...]
    pushed[...] = (grad[...] * query[...]).astype(jnp.bfloat16)
    lanes = lane_group()
    row = lax.broadcasted_iota(jnp.int32, (LONG, 2 * LONG), 0)
    begins = jnp.broadcast_to(starts[...], (LONG, 2 * LONG))
    same = row >= begins
    later = (row + LONG >= begins)[:, LONG:]
    earlier = (row - LONG >= begins)[:, :LONG]
    before = jnp.zeros((LONG, WIDTH), jnp.float32)
    for group in range(GROUPS):
        skew = skewed(table, group)
        both = jnp.where(same, skew, 0.0).astype(jnp.bfloat16)
        found = jnp.dot(both, pushed[...], preferred_element_type=jnp.float32)
        own[:LONG] = found if group == 0 else jnp.where(lanes == group, found, own[:LONG])
        second = jnp.where(later, skew[:, :LONG], 0.0).astype(jnp.bfloat16)
        found = jnp.dot(second, pushed[LONG:], preferred_element_type=jnp.float32)
        own[LONG:] = found if group == 0 else jnp.where(lanes == group, found, own[LONG:])
        first = jnp.where(earlier, skew[:, LONG:], 0.0).astype(jnp.bfloat16)
        found = jnp.dot(first, pushed[:LONG], preferred_element_type=jnp.float32)
        before = jnp.where(lanes == group, found, before)
    leaving[:LONG] = before.astype(jnp.bfloat16)
    limits[:8] = jnp.full((8, WIDTH), -1, jnp.int32)
    limits[8:] = spans[:8]
    small[:8] = jnp.zeros((8, WIDTH), jnp.float32)
    heads = []
    for stream in range(3):
        if stream == 0:
            small[8:] = grad_query[:8]
        else:
            small[8:] = own[:8] * (value[:8] if stream == 1 else key[:8])
        total = jnp.zeros((8, WIDTH), jnp.float32)
        for tap in range(TAPS):
            weighted = taps[stream, tap : tap + 1, :] * small[tap : tap + 8]
            total = total + jnp.where(limits[tap : tap + 8] >= tap, weighted, 0.0)
        heads.append(total)
    heads.append(jnp.zeros((8, WIDTH), jnp.float32))
    leaving[LONG:] = jnp.concatenate(heads).astype(jnp.bfloat16)


def rim_kernel(query, key, value, out):
    out[:RIM] = key[ROWS - RIM :]
    out[RIM : 2 * RIM] = value[ROWS - RIM :]
    out[2 * RIM :] = query[ROWS - 16 :]


def stream_kernel(grad_query, own, came, key, value, taps, spans, out, source, limits):
    limits[:ROWS] = spans[...]
    limits[ROWS:] = jnp.full((8, WIDTH), -1, jnp.int32)
    source[ROWS:] = jnp.zeros((8, WIDTH), jnp.float32)
    tail = came[LONG:].astype(jnp.float32)
    for stream in range(3):
        if stream == 0:
            source[:ROWS] = grad_query[...]
        else:
            other = value if stream == 1 else key
            source[:LONG] = own[:LONG] * other[:LONG]
            source[LONG:ROWS] = (own[LONG:] + came[:LONG].astype(jnp.float32)) * other[LONG:]
        for top in range(0, ROWS, STRIP):
            strip = tap_sum(source, limits, taps, stream, top, STRIP, 1)
            if top + STRIP == ROWS:
                extra = jnp.zeros((STRIP - 8, WIDTH), jnp.float32)
                extra = jnp.concatenate([extra, tail[stream * 8 : stream * 8 + 8]])
                strip = strip + extra
            out[stream, top : top + STRIP] = strip.astype(jnp.bfloat16)


def wide(rows):
    return jax.ShapeDtypeStruct((rows, WIDTH), jnp.float32)


def narrow(*shape):
    return jax.ShapeDtypeStruct(shape, jnp.bfloat16)


def vmem(rows, kind):
    return pltpu.VMEM((rows, WIDTH), kind)


def run_rim(*streams):
    return pl.pallas_call(rim_kernel, out_shape=narrow(2 * RIM + 16, WIDTH))(*streams)


def run_forward(*arrays):
    return pl.pallas_call(
        forward_kernel,
        out_shape=[wide(ROWS)] * 4
        + [narrow(ROWS, WIDTH), jax.ShapeDtypeStruct((ROWS, WIDTH), jnp.int32)],
        scratch_shapes=[
            vmem(ROWS + 16, jnp.float32),
            vmem(ROWS + RIM, jnp.float32),
            vmem(ROWS + RIM, jnp.float32),
            vmem(ROWS + RIM, jnp.int32),
            vmem(ROWS + LONG, jnp.bfloat16),
        ],
    )(*arrays)


def run_backward(*arrays):
    return pl.pallas_call(
        backward_kernel,
        out_shape=[wide(ROWS), wide(ROWS), narrow(LONG + 32, WIDTH)],
        scratch_shapes=[
            vmem(ROWS, jnp.bfloat16),
            vmem(16, jnp.float32),
            vmem(16, jnp.int32),
        ],
    )(*arrays)


def run_streams(*arrays):
    return pl.pallas_call(
        stream_kernel,
        out_shape=narrow(3, ROWS, WIDTH),
        scratch_shapes=[vmem(ROWS + 8, jnp.float32), vmem(ROWS + 8, jnp.int32)],
    )(*arrays)


RING = 8
SHARE = 4


def tp_move(value, dy=0, flip_x=0, flip_core=0):
    pairs = []
    for source in range(RING * SHARE):
        ring_pos, side, core = (source // SHARE, source // 2 % 2, source % 2)
        target = (ring_pos + dy) % RING * SHARE + (side ^ flip_x) * 2 + (core ^ flip_core)
        pairs.append((source, target))
    return lax.ppermute(value, "tp", pairs)


def meet(*values):
    return lax.optimization_barrier(values)


def onward(value):
    pairs = []
    for source in range(RING * SHARE):
        step = 1 if source % 2 == 0 else RING - 1
        pairs.append((source, (source + step * SHARE) % (RING * SHARE)))
    return lax.ppermute(value, "tp", pairs)


def widen(value):
    return value.astype(jnp.float32)


def join(block, arrived):
    return (widen(block) + widen(arrived)).astype(jnp.bfloat16)


def owners(rows, side, core):
    place = jnp.arange(rows * 2 * RING, dtype=jnp.int32)
    ring_pos, far = (place // (2 * rows), place // rows % 2)
    return ring_pos * 4 * rows + (far ^ side) * 2 * rows + core * rows + place % rows


def arrivals(rows, ring_pos, side, core):
    token = jnp.arange(rows * 4 * RING, dtype=jnp.int32)
    block, row = (token // rows, token % rows)
    other, far = (block % 2 ^ core, block // 2 % 2 ^ side)
    step = jnp.where(core == 0, ring_pos - block // 4, block // 4 - ring_pos) % RING
    mine = jnp.logical_or(step < 4, jnp.logical_and(step == 4, other == 0))
    here = jnp.where(step == 4, 32, step * 4 + other * 2) + far
    there = jnp.where(step == 4, 34, (RING - step) * 4 + (1 - other) * 2 + 16) + far
    return jnp.where(mine, here, there) * rows + row


def body(
    query_stream,
    key_stream,
    value_stream,
    short_filter,
    long_filter,
    doc_start,
    out_weight,
    out_cotangent,
):
    tok_rows = query_stream.shape[0]
    member = lax.axis_index("tp")
    ring_pos, side, core = (member // SHARE, member // 2 % 2, member % 2)
    own_rows = tok_rows // (RING * SHARE)
    rim_rows = run_rim(query_stream, key_stream, value_stream)
    before = shifted(rim_rows, "ctx", 1)
    begins = (doc_start - lax.axis_index("ctx") * tok_rows)[None]
    cross = tp_move(out_cotangent, flip_x=1)
    pair = jnp.concatenate([out_cotangent, cross])
    quad = jnp.concatenate([pair, tp_move(pair, flip_core=1)])
    step1 = onward(quad)
    query_short, key_short, value_short, filtered, gated, spans = run_forward(
        before, query_stream, key_stream, value_stream, short_filter, long_filter, begins
    )
    step2 = onward(step1)
    token = jnp.arange(tok_rows, dtype=jnp.int32)
    half = tok_rows // 2
    mine = owners(own_rows, side, core)
    others = owners(own_rows, side, 1 - core)
    pick = jnp.concatenate([mine, others])[:, None] == token[None, :]
    ordered = jnp.dot(
        pick.astype(jnp.bfloat16), gated, preferred_element_type=jnp.float32
    ).astype(jnp.bfloat16)
    away = jnp.dot(ordered[half:], out_weight, preferred_element_type=jnp.float32)
    received = tp_move(away.astype(jnp.bfloat16), flip_core=1)
    here = jnp.dot(ordered[:half], out_weight, preferred_element_type=jnp.float32)
    parts = (here + widen(received)).astype(jnp.bfloat16)
    rings = [[place * SHARE + share for place in range(RING)] for share in range(SHARE)]
    sums = lax.psum_scatter(
        parts, "tp", scatter_dimension=0, axis_index_groups=rings, tiled=True
    )
    step3 = onward(step2)
    step4 = onward(step3[: 2 * own_rows])
    gathered = jnp.concatenate([quad, step1, step2, step3])
    sibling = tp_move(gathered, flip_core=1)
    last = jnp.concatenate([step4, tp_move(step4, flip_core=1)])
    dims = (((1,), (1,)), ((), ()))
    grads = []
    for block in (gathered, sibling, last):
        grads.append(lax.dot_general(block, out_weight, dims, preferred_element_type=jnp.float32))
    slots = jnp.arange(36 * own_rows, dtype=jnp.int32)
    place = arrivals(own_rows, ring_pos, side, core)[:, None] == slots[None, :]
    grad_gated = jnp.dot(
        place.astype(jnp.float32),
        jnp.concatenate(grads),
        precision=lax.Precision.HIGHEST,
        preferred_element_type=jnp.float32,
    )
    grad_query, own_mixed, outgoing = run_backward(
        grad_gated,
        filtered,
        query_short,
        key_short,
        value_short,
        short_filter,
        long_filter,
        begins,
        spans,
    )
    from_next = shifted(outgoing, "ctx", -1)
    sums, _ = meet(sums, outgoing)
    partner = tp_move(sums[own_rows:], flip_x=1)
    projected = join(sums[:own_rows], partner)
    stream_grads = run_streams(
        grad_query, own_mixed, from_next, key_short, value_short, short_filter, spans
    )
    return (projected, stream_grads)


def solution(mesh):
    in_specs = (
        P("ctx", "tp"),
        P("ctx", "tp"),
        P("ctx", "tp"),
        P(None, None, "tp"),
        P("tp", None),
        P("ctx"),
        P("tp", None),
        P(("ctx", "tp"), None),
    )
    out_specs = (P(("ctx", "tp"), None), P(None, "ctx", "tp"))
    return jax.shard_map(body, mesh=mesh, in_specs=in_specs, out_specs=out_specs, check_vma=False)
```
